512 devices in a mesh: dp: 8 (over y_lo, core), ctx: 64 (over x, y_hi, z).
Axes of the slice: x: 4, y: 8 (y_hi: 2, y_lo: 4; y = y_hi * 4 + y_lo), z: 8, core: 2. Of those that a mesh axis runs over, the one named last changes fastest.
Arguments:
- tokens: bfloat16 [8, 32768, 1024], P('dp', 'ctx'), may hold values from -6 to 6
- w_query: bfloat16 [1024, 1024], P('dp')
- w_key: bfloat16 [1024, 1024], P('dp')
- w_value: bfloat16 [1024, 1024], P('dp'), may hold values from -0.1875 to 0.1875
- w_output: bfloat16 [1024, 1024], P('dp'), may hold values from -0.1875 to 0.1875
- nbr_index: int32 [8, 256, 8], P('dp', 'ctx'), may hold values from 0 to 255, as said below
- nbr_count: int32 [8, 256], P('dp', 'ctx'), may hold values from 1 to 8, as said below
Outputs:
- update: bfloat16 [8, 32768, 1024], P('dp', 'ctx')
The draws below stay inside these ranges and needn't reach their ends.
Inputs may be any that keep to these rules, and one draw needn't show every extreme that they name: `nbr_index`: in each row the first nbr_count slots name distinct blocks, slot 0 names the query block itself, and every slot names a block at most 8 blocks away from it; unused slots name blocks of that same range. In every draw some block is exactly 8 away from a query block that uses it. `nbr_count`: in every draw some query block uses all 8 slots.
All inputs are finite; a program needn't handle non-finite values.
Results may differ from the reference program's by a relative error of at most 0.0089.
Values may be sent and summed in bfloat16 or wider, within the bound.
No kernel may reach another device: no remote copies, remote signals or barrier semaphores. Data moves between devices by JAX's collectives and lax.ppermute only.
A program may use at most 128 MiB of HBM per device.

```python
import jax
import jax.numpy as jnp
from jax import lax

D = 1024
HEADS = 8
HD = 128
BLK = 128
MAXN = 8
REACH = 2
BPD = 4
NBLK = 256
TOKENS = 32768
SAMPLES = 8


def projection_pair(key):
    first = jax.random.normal(jax.random.fold_in(key, 11), (D, D), jnp.float32) * D ** (-0.5)
    second = jax.random.normal(jax.random.fold_in(key, 12), (D, D), jnp.float32) * D ** (-0.5)
    query_w = first
    key_w = second
    return (query_w, key_w)


def draw_w_query(key, part):
    return projection_pair(key)[0].astype(jnp.bfloat16)


def draw_w_key(key, part):
    return projection_pair(key)[1].astype(jnp.bfloat16)


def one_list(key):
    span = REACH * BPD
    offsets = jnp.concatenate([jnp.arange(-span, 0, dtype=jnp.int32), jnp.arange(1, span + 1, dtype=jnp.int32)])
    row_keys = jax.random.split(jax.random.fold_in(key, 5), NBLK)
    perms = jax.vmap(lambda one_key: jax.random.permutation(one_key, 2 * span))(row_keys)
    cand = jnp.take(offsets, perms)
    rows = jnp.arange(NBLK, dtype=jnp.int32)
    target = rows[:, None] + cand
    invalid = ((target < 0) | (target >= NBLK)).astype(jnp.int32)
    forced = jax.random.randint(jax.random.fold_in(key, 7), (), 0, NBLK, dtype=jnp.int32)
    far = jnp.where(forced + span < NBLK, span, -span)
    special = (rows[:, None] == forced) & (cand == far)
    position = jnp.arange(2 * span, dtype=jnp.int32)[None, :] + 1
    sortkey = invalid * (4 * span + 8) + jnp.where(special, 0, position)
    order = jnp.argsort(sortkey, axis=1, stable=True)
    chosen = jnp.take_along_axis(target, order, axis=1)[:, :MAXN - 1]
    index = jnp.concatenate([rows[:, None], chosen], axis=1).astype(jnp.int32)
    heavy_dev = jax.random.randint(jax.random.fold_in(key, 9), (NBLK // BPD,), 0, 4, dtype=jnp.int32) == 0
    heavy = jnp.take(heavy_dev, rows // BPD)
    high = jax.random.randint(jax.random.fold_in(key, 13), (NBLK,), MAXN - 2, MAXN + 1, dtype=jnp.int32)
    low = jax.random.randint(jax.random.fold_in(key, 17), (NBLK,), 1, MAXN // 2 + 1, dtype=jnp.int32)
    count = jnp.where(heavy, high, low)
    count = jnp.where(rows == forced, MAXN, count).astype(jnp.int32)
    return (index, count)


def neighbour_lists(key):
    sample_keys = jax.random.split(jax.random.fold_in(key, 3), SAMPLES)
    return jax.vmap(one_list)(sample_keys)


def draw_nbr_index(key, part):
    return neighbour_lists(key)[0]


def draw_nbr_count(key, part):
    return neighbour_lists(key)[1]


def steps_of(own_key, extent, pieces, least, high):
    def one(axis_at, parts):
        steps = jax.random.uniform(jax.random.fold_in(jax.random.fold_in(own_key, 6), axis_at), (parts,), jnp.float32, least / len(pieces), high / len(pieces))
        return jnp.repeat(jnp.exp(steps), extent[axis_at] // parts).reshape((-1,) + (1,) * (len(extent) - axis_at - 1))

    level = one(*pieces[0])
    for cut in pieces[1:]:
        level = level * one(*cut)
    return level


def bell_draw(key, shape, spread, limit, shards=(), kind=jnp.bfloat16):
    entries = spread * jax.random.normal(key, shape, jnp.float32)
    if shards:
        entries = entries * steps_of(key, shape, shards, -0.22, 0.18)
    return jnp.clip(entries, -limit, limit).astype(kind)


def setup_inputs(seed: int = 0) -> dict:
    splits = jax.random.split(jax.random.key(seed), 8)
    tokens = bell_draw(splits[0], (SAMPLES, TOKENS, D), 1.0, 6.0, ((0, 8), (1, 64)))
    w_query = draw_w_query(jax.random.fold_in(splits[7], 71), 0)
    w_key = draw_w_key(jax.random.fold_in(splits[7], 71), 0)
    w_value = bell_draw(splits[3], (D, D), D ** -0.5, 0.1875, ((0, 8),))
    w_output = bell_draw(splits[4], (D, D), D ** -0.5, 0.1875, ((0, 8),))
    nbr_index = draw_nbr_index(jax.random.fold_in(splits[7], 71), 0)
    nbr_count = draw_nbr_count(jax.random.fold_in(splits[7], 71), 0)
    return dict(tokens=tokens, w_query=w_query, w_key=w_key, w_value=w_value, w_output=w_output, nbr_index=nbr_index, nbr_count=nbr_count)


def attend_block(query_blk, key_sel, value_sel, used):
    query_heads = query_blk.reshape(BLK, HEADS, HD).astype(jnp.float32)
    key_heads = key_sel.reshape(MAXN * BLK, HEADS, HD).astype(jnp.float32)
    value_heads = value_sel.reshape(MAXN * BLK, HEADS, HD).astype(jnp.float32)
    scores = jnp.einsum('qhd,khd->hqk', query_heads, key_heads) * HD ** (-0.5)
    slot_used = jnp.arange(MAXN * BLK) // BLK < used
    scores = jnp.where(slot_used[None, None, :], scores, -1e+30)
    peak = lax.optimization_barrier(jnp.max(scores, axis=-1, keepdims=True))
    expo = jnp.exp(scores - peak) * slot_used[None, None, :].astype(jnp.float32)
    weights = (expo / lax.optimization_barrier(jnp.sum(expo, axis=-1, keepdims=True))).astype(jnp.bfloat16)
    attended = jnp.einsum('hqk,khd->qhd', weights.astype(jnp.float32), value_heads)
    return attended.reshape(BLK, HEADS * HD).astype(jnp.bfloat16)

def one_sample(tokens, w_query, w_key, w_value, w_output, nbr_index, nbr_count):
    values_f = tokens.astype(jnp.float32)
    normed = (values_f * lax.rsqrt(lax.optimization_barrier(jnp.mean(values_f * values_f, axis=-1, keepdims=True)) + 1e-05)).astype(jnp.bfloat16)
    queries = jnp.dot(normed, w_query, preferred_element_type=jnp.float32).astype(jnp.bfloat16)
    keys = jnp.dot(normed, w_key, preferred_element_type=jnp.float32).astype(jnp.bfloat16)
    values = jnp.dot(normed, w_value, preferred_element_type=jnp.float32).astype(jnp.bfloat16)
    key_blocks = keys.reshape(NBLK, BLK, HEADS * HD)
    value_blocks = values.reshape(NBLK, BLK, HEADS * HD)
    query_blocks = queries.reshape(NBLK, BLK, HEADS * HD)

    def per_block(items):
        query_blk, index_row, used = items
        return attend_block(query_blk, key_blocks[index_row], value_blocks[index_row], used)
    attended = lax.map(per_block, (query_blocks, nbr_index, nbr_count)).reshape(NBLK * BLK, HEADS * HD)
    return jnp.dot(attended, w_output, preferred_element_type=jnp.float32).astype(jnp.bfloat16)

def reference(tokens, w_query, w_key, w_value, w_output, nbr_index, nbr_count):

    def per_sample(items):
        sample_tok, index_all, count_all = items
        return one_sample(sample_tok, w_query, w_key, w_value, w_output, index_all, count_all)
    return lax.map(per_sample, (tokens, nbr_index, nbr_count))
```

```python
import numpy as np
import jax
import jax.numpy as jnp
from jax import lax
from jax.experimental import pallas as pl
from jax.experimental.pallas import tpu as pltpu
from jax.sharding import PartitionSpec as P

D = 1024
HEADS = 8
HD = 128
BLK = 128
MAXN = 8
REACH = 2
ROWS = 512
NDP = 8
NCTX = 64
BF = jnp.bfloat16
F32 = jnp.float32
SCALE2 = float(HD ** (-0.5) * np.log2(np.e))
VMEM_LIMIT = 60 << 20
AXES = ("dp", "ctx")


def flat(x, y, z, core):
    return ((y % 4) * 2 + core) * NCTX + (x % 4) * 16 + ((y % 8) // 4) * 8 + z % 8


def coords(index):
    dp, ctx = divmod(index, NCTX)
    return ctx // 16, (ctx // 8 % 2) * 4 + dp // 2, ctx % 8, dp % 2


def routes(target):
    return [(i, flat(*target(*coords(i)))) for i in range(NDP * NCTX)]


def ctx_routes(step, keep=lambda r: True):
    return [
        (dp * NCTX + r, dp * NCTX + r + step)
        for dp in range(NDP)
        for r in range(NCTX)
        if 0 <= r + step < NCTX and keep(r)
    ]


FROM_UP = routes(lambda x, y, z, c: (x, y - 1, z, c))
FROM_DOWN = routes(lambda x, y, z, c: (x, y + 1, z, c))
FROM_FAR = routes(lambda x, y, z, c: (x, y + 2 if y % 2 == 0 else y - 2, z, c))
SHIFTS = (1, -1, 2)
X_NEXT = routes(lambda x, y, z, c: (x + 1, y, z, c))
X_PREV = routes(lambda x, y, z, c: (x - 1, y, z, c))
SIBLING = routes(lambda x, y, z, c: (x, y, z, 1 - c))


def send(value, pairs):
    return lax.ppermute(value, AXES, pairs)


def normalise(tok):
    v = tok.astype(F32)
    return (v * lax.rsqrt(jnp.mean(v * v, axis=-1, keepdims=True) + 1e-05)).astype(BF)


def piece_copies(pos, srcs, picks, dst, sem):
    ylo, core, par = pos[0], pos[1], pos[2]
    own, sib, mine, other, sib_mine, sib_other = srcs
    copies = []

    def add(src, row, n, col):
        copies.append(
            pltpu.make_async_copy(
                src, dst.at[pl.ds(pl.multiple_of(row, 64), n), pl.ds(col, D)], sem
            )
        )

    for at, w in enumerate(picks):
        add(own.at[w], (ylo * 2 + core) * 128, 128, at * D)
        add(sib.at[w], (ylo * 2 + 1 - core) * 128, 128, at * D)
        for i, s in enumerate(SHIFTS):
            base = lax.rem(ylo + s + 4, 4) * 2
            row = (base + core) * 128
            row_sib = (base + 1 - core) * 128
            add(mine.at[i, w], row + par * 64, 64, at * D)
            add(other.at[i, w % 2], row + (1 - par) * 64, 64, at * D)
            add(sib_mine.at[i, w], row_sib + par * 64, 64, at * D)
            add(sib_other.at[i, w % 2], row_sib + (1 - par) * 64, 64, at * D)
    return copies


def first_proj_kernel(pos, tok, *refs):
    srcs, (out, w_out, w_buf, sem, sem2) = refs[:6], refs[6:]
    copies = piece_copies(pos, srcs, (0, 1), w_buf, sem)
    for c in copies:
        c.start()
    for c in copies:
        c.wait()
    save = pltpu.make_async_copy(w_buf, w_out, sem2)
    save.start()
    for i in range(0, ROWS, 256):
        rows = slice(i, i + 256)
        out[rows, :] = jnp.dot(
            normalise(tok[rows, :]), w_buf[...], preferred_element_type=F32
        ).astype(BF)
    save.wait()


def proj_kernel(tok, w, out):
    out[...] = jnp.dot(normalise(tok[...]), w[...], preferred_element_type=F32).astype(BF)


def query_kernel(pos, tok, *refs):
    srcs, (out, w_out, w_buf, sem, sem2) = refs[:6], refs[6:]
    copies = piece_copies(pos, srcs, (2, 3), w_buf, sem)
    for c in copies:
        c.start()
    for c in copies:
        c.wait()
    save = pltpu.make_async_copy(w_buf.at[:, pl.ds(D, D)], w_out, sem2)
    save.start()
    out[...] = jnp.dot(
        normalise(tok[...]), w_buf[:, :D], preferred_element_type=F32
    ).astype(BF)
    save.wait()


def final_kernel(
    idx, cnt, low2, up2, query, w_kv, w_o, kv_low, kv_own, kv_up, out, kv, w_buf, wo_buf, att, sem
):
    get_w = pltpu.make_async_copy(w_kv, w_buf, sem.at[0])
    get_w.start()
    gets = [
        pltpu.make_async_copy(src, kv.at[pl.ds((i + 1) * ROWS, ROWS)], sem.at[1 + i])
        for i, src in enumerate((kv_low, kv_own, kv_up))
    ]
    gets.append(pltpu.make_async_copy(w_o, wo_buf, sem.at[4]))
    for g in gets:
        g.start()
    get_w.wait()
    for tok, base in ((low2, 0), (up2, 4 * ROWS)):
        for i in range(0, ROWS, 256):
            kv[base + i : base + i + 256, :] = jnp.dot(
                normalise(tok[i : i + 256, :]), w_buf[...], preferred_element_type=F32
            ).astype(BF)
    for g in gets:
        g.wait()

    def one_block(b, carry):
        used = cnt[b]
        rows = pl.ds(pl.multiple_of(b * BLK, BLK), BLK)
        starts = [pl.multiple_of(idx[b, j] * BLK, BLK) for j in range(MAXN)]
        for h in range(HEADS):
            hs = pl.ds(h * HD, HD)
            q = query[rows, hs]
            scores = []
            for j in range(MAXN):
                s = lax.dot_general(
                    q, kv[pl.ds(starts[j], BLK), hs], (((1,), (1,)), ((), ())),
                    preferred_element_type=F32,
                )
                scores.append(jnp.where(j < used, s, -1e30))
            peak = scores[0]
            for s in scores[1:]:
                peak = jnp.maximum(peak, s)
            peak = jnp.max(peak, axis=-1, keepdims=True)
            expo = [jnp.exp2((s - peak) * SCALE2) for s in scores]
            total = expo[0]
            for e in expo[1:]:
                total = total + e
            total = jnp.sum(total, axis=-1, keepdims=True)
            acc = jnp.zeros((BLK, HD), F32)
            for j in range(0, MAXN, 2):
                vals = jnp.concatenate(
                    [kv[pl.ds(starts[i], BLK), pl.ds(D + h * HD, HD)] for i in (j, j + 1)], axis=0
                )
                wts = jnp.concatenate([expo[j].astype(BF), expo[j + 1].astype(BF)], axis=1)
                acc = acc + jnp.dot(wts, vals, preferred_element_type=F32)
            att[rows, hs] = (acc / total).astype(BF)
        return carry

    lax.fori_loop(0, ROWS // BLK, one_block, 0)
    for i in range(0, ROWS, 256):
        out[i : i + 256, :] = jnp.dot(
            att[i : i + 256, :], wo_buf[...], preferred_element_type=F32
        ).astype(BF)


def body(tokens, w_query, w_key, w_value, w_output, nbr_index, nbr_count):
    tok = tokens[0]
    dp = lax.axis_index("dp")
    rank = lax.axis_index("ctx")
    ylo, core, par = dp // 2, dp % 2, (rank // 16) % 2
    pos = jnp.stack([ylo, core, par]).astype(jnp.int32)

    up, down = ctx_routes(1), ctx_routes(-1)
    own = jnp.stack([w_key, w_value, w_query, w_output])
    half = lax.dynamic_slice_in_dim(own, par * 64, 64, axis=1)
    mine = jnp.stack([send(half, p) for p in (FROM_UP, FROM_DOWN, FROM_FAR)])
    low = send(tok, up)
    high = send(tok, down)
    sib = send(own, SIBLING)
    other_kv = send(mine[:, :2], X_NEXT)
    other_qo = send(mine[:, 2:], X_PREV)
    sib_mine = send(mine, SIBLING)
    sib_kv = send(other_kv, SIBLING)
    sib_qo = send(other_qo, SIBLING)
    low2 = send(low, up)
    high2 = send(high, down)

    vm = pl.BlockSpec(memory_space=pltpu.VMEM)
    anyspace = pl.BlockSpec(memory_space=pl.ANY)
    smem = pl.BlockSpec(memory_space=pltpu.SMEM)
    params = pltpu.CompilerParams(vmem_limit_bytes=VMEM_LIMIT)
    pieces_kv = (own, sib, mine, other_kv, sib_mine, sib_kv)
    pieces_qo = (own, sib, mine, other_qo, sib_mine, sib_qo)
    kv_own, w_kv = pl.pallas_call(
        first_proj_kernel,
        in_specs=[smem, vm] + [anyspace] * 6,
        out_specs=[vm, anyspace],
        out_shape=[
            jax.ShapeDtypeStruct((ROWS, 2 * D), BF),
            jax.ShapeDtypeStruct((D, 2 * D), BF),
        ],
        scratch_shapes=[
            pltpu.VMEM((D, 2 * D), BF),
            pltpu.SemaphoreType.DMA,
            pltpu.SemaphoreType.DMA,
        ],
        compiler_params=params,
        name="first_proj",
    )(pos, tok, *pieces_kv)

    def project(t):
        return pl.pallas_call(
            proj_kernel,
            grid=(2,),
            in_specs=[
                pl.BlockSpec((256, D), lambda i: (i, 0)),
                pl.BlockSpec((D, 2 * D), lambda i: (0, 0), pipeline_mode=pl.Buffered(1)),
            ],
            out_specs=pl.BlockSpec((256, 2 * D), lambda i: (i, 0)),
            out_shape=jax.ShapeDtypeStruct((ROWS, 2 * D), BF),
            compiler_params=params,
            name="proj",
        )(t, w_kv)

    kv_low = project(low)
    kv_high = project(high)
    query, w_o = pl.pallas_call(
        query_kernel,
        in_specs=[smem, vm] + [anyspace] * 6,
        out_specs=[vm, anyspace],
        out_shape=[jax.ShapeDtypeStruct((ROWS, D), BF), jax.ShapeDtypeStruct((D, D), BF)],
        scratch_shapes=[
            pltpu.VMEM((D, 2 * D), BF),
            pltpu.SemaphoreType.DMA,
            pltpu.SemaphoreType.DMA,
        ],
        compiler_params=params,
        name="query",
    )(pos, tok, *pieces_qo)
    index = nbr_index[0] - (rank * (ROWS // BLK) - REACH * (ROWS // BLK))
    update = pl.pallas_call(
        final_kernel,
        in_specs=[smem, smem, vm, vm, vm] + [anyspace] * 5,
        out_specs=vm,
        out_shape=jax.ShapeDtypeStruct((ROWS, D), BF),
        scratch_shapes=[
            pltpu.VMEM((5 * ROWS, 2 * D), BF),
            pltpu.VMEM((D, 2 * D), BF),
            pltpu.VMEM((D, D), BF),
            pltpu.VMEM((ROWS, D), BF),
            pltpu.SemaphoreType.DMA((5,)),
        ],
        compiler_params=params,
        name="final",
    )(index, nbr_count[0], low2, high2, query, w_kv, w_o, kv_low, kv_own, kv_high)
    return update[None]


def solution(mesh):
    placed = (
        P("dp", "ctx", None),
        P("dp", None),
        P("dp", None),
        P("dp", None),
        P("dp", None),
        P("dp", "ctx", None),
        P("dp", "ctx"),
    )
    return jax.shard_map(
        body, mesh=mesh, in_specs=placed, out_specs=P("dp", "ctx", None), check_vma=False
    )
```

```python
import numpy as np
import jax
import jax.numpy as jnp
from jax import lax
from jax.experimental import pallas as pl
from jax.experimental.pallas import tpu as pltpu
from jax.sharding import PartitionSpec as P

D = 1024
HEADS = 8
HD = 128
BLK = 128
MAXN = 8
REACH = 2
ROWS = 512
NDP = 8
NCTX = 64
BF = jnp.bfloat16
F32 = jnp.float32
SCALE2 = float(HD ** (-0.5) * np.log2(np.e))
VMEM_LIMIT = 60 << 20
AXES = ("dp", "ctx")


def flat(x, y, z, core):
    return ((y % 4) * 2 + core) * NCTX + (x % 4) * 16 + ((y % 8) // 4) * 8 + z % 8


def coords(index):
    dp, ctx = divmod(index, NCTX)
    return ctx // 16, (ctx // 8 % 2) * 4 + dp // 2, ctx % 8, dp % 2


def routes(target):
    return [(i, flat(*target(*coords(i)))) for i in range(NDP * NCTX)]


def ctx_routes(step, keep=lambda r: True):
    return [
        (dp * NCTX + r, dp * NCTX + r + step)
        for dp in range(NDP)
        for r in range(NCTX)
        if 0 <= r + step < NCTX and keep(r)
    ]


FROM_UP = routes(lambda x, y, z, c: (x, y - 1, z, c))
FROM_DOWN = routes(lambda x, y, z, c: (x, y + 1, z, c))
FROM_FAR = routes(lambda x, y, z, c: (x, y + 2 if y % 2 == 0 else y - 2, z, c))
SHIFTS = (1, -1, 2)
X_NEXT = routes(lambda x, y, z, c: (x + 1, y, z, c))
X_PREV = routes(lambda x, y, z, c: (x - 1, y, z, c))
SIBLING = routes(lambda x, y, z, c: (x, y, z, 1 - c))


def send(value, pairs):
    return lax.ppermute(value, AXES, pairs)


def normalise(tok):
    v = tok.astype(F32)
    return (v * lax.rsqrt(jnp.mean(v * v, axis=-1, keepdims=True) + 1e-05)).astype(BF)


def piece_copies(pos, srcs, picks, dst, sem):
    ylo, core, par = pos[0], pos[1], pos[2]
    own, sib, mine, other, sib_mine, sib_other = srcs
    copies = []

    def add(src, row, n, col):
        copies.append(
            pltpu.make_async_copy(
                src, dst.at[pl.ds(pl.multiple_of(row, 64), n), pl.ds(col, D)], sem
            )
        )

    for at, w in enumerate(picks):
        add(own.at[w], (ylo * 2 + core) * 128, 128, at * D)
        add(sib.at[w], (ylo * 2 + 1 - core) * 128, 128, at * D)
        for i, s in enumerate(SHIFTS):
            base = lax.rem(ylo + s + 4, 4) * 2
            row = (base + core) * 128
            row_sib = (base + 1 - core) * 128
            add(mine.at[i, w], row + par * 64, 64, at * D)
            add(other.at[i, w % 2], row + (1 - par) * 64, 64, at * D)
            add(sib_mine.at[i, w], row_sib + par * 64, 64, at * D)
            add(sib_other.at[i, w % 2], row_sib + (1 - par) * 64, 64, at * D)
    return copies


def first_proj_kernel(pos, tok, *refs):
    srcs, (out, w_out, w_buf, sem, sem2) = refs[:6], refs[6:]
    copies = piece_copies(pos, srcs, (0, 1), w_buf, sem)
    for c in copies:
        c.start()
    for c in copies:
        c.wait()
    save = pltpu.make_async_copy(w_buf, w_out, sem2)
    save.start()
    for i in range(0, ROWS, 256):
        rows = slice(i, i + 256)
        out[rows, :] = jnp.dot(
            normalise(tok[rows, :]), w_buf[...], preferred_element_type=F32
        ).astype(BF)
    save.wait()


def pair_kernel(high, low, w, out):
    tok = jnp.where(pl.program_id(0) < 2, high[...], low[...])
    out[...] = jnp.dot(normalise(tok), w[...], preferred_element_type=F32).astype(BF)


def query_kernel(pos, tok, *refs):
    srcs, (out, w_out, w_buf, sem, sem2) = refs[:6], refs[6:]
    copies = piece_copies(pos, srcs, (2, 3), w_buf, sem)
    for c in copies:
        c.start()
    for c in copies:
        c.wait()
    save = pltpu.make_async_copy(w_buf.at[:, pl.ds(D, D)], w_out, sem2)
    save.start()
    out[...] = jnp.dot(
        normalise(tok[...]), w_buf[:, :D], preferred_element_type=F32
    ).astype(BF)
    save.wait()


def final_kernel(
    idx, cnt, low2, up2, query, w_kv, w_o, kv_pair, kv_own, out, kv, w_buf, wo_buf, att, score, sem
):
    get_w = pltpu.make_async_copy(w_kv, w_buf, sem.at[0])
    get_w.start()
    gets = [
        pltpu.make_async_copy(kv_pair.at[pl.ds(ROWS, ROWS)], kv.at[pl.ds(ROWS, ROWS)], sem.at[1]),
        pltpu.make_async_copy(kv_own, kv.at[pl.ds(2 * ROWS, ROWS)], sem.at[2]),
        pltpu.make_async_copy(kv_pair.at[pl.ds(0, ROWS)], kv.at[pl.ds(3 * ROWS, ROWS)], sem.at[3]),
    ]
    gets.append(pltpu.make_async_copy(w_o, wo_buf, sem.at[4]))
    for g in gets:
        g.start()
    get_w.wait()
    for tok, base in ((low2, 0), (up2, 4 * ROWS)):
        for i in range(0, ROWS, 256):
            kv[base + i : base + i + 256, :] = jnp.dot(
                normalise(tok[i : i + 256, :]), w_buf[...], preferred_element_type=F32
            ).astype(BF)
    for g in gets:
        g.wait()

    def one_block(b, carry):
        used = cnt[b]
        rows = pl.ds(pl.multiple_of(b * BLK, BLK), BLK)
        starts = [
            pl.multiple_of(jnp.where(j < used, idx[b, j], idx[b, 0]) * BLK, BLK)
            for j in range(MAXN)
        ]
        bias = [jnp.where(j < used, 0.0, -1e30) for j in range(MAXN)]
        for h in range(HEADS):
            hs = pl.ds(h * HD, HD)
            q = query[rows, hs]
            for j in range(MAXN):
                score[h, :, j * BLK : (j + 1) * BLK] = lax.dot_general(
                    q, kv[pl.ds(starts[j], BLK), hs], (((1,), (1,)), ((), ())),
                    preferred_element_type=F32,
                )
        for h in range(HEADS):
            hs = pl.ds(h * HD, HD)
            scores = [score[h, :, j * BLK : (j + 1) * BLK] for j in range(MAXN)]
            peak = scores[0]
            for s in scores[1:]:
                peak = jnp.maximum(peak, s)
            peak = jnp.max(peak, axis=-1, keepdims=True)
            expo = [jnp.exp2((s - (peak - off)) * SCALE2) for s, off in zip(scores, bias)]
            total = expo[0]
            for e in expo[1:]:
                total = total + e
            total = jnp.sum(total, axis=-1, keepdims=True)
            acc = None
            for j in range(0, MAXN, 2):
                vals = jnp.concatenate(
                    [kv[pl.ds(starts[i], BLK), pl.ds(D + h * HD, HD)] for i in (j, j + 1)], axis=0
                )
                wts = jnp.concatenate([expo[j].astype(BF), expo[j + 1].astype(BF)], axis=1)
                part = jnp.dot(wts, vals, preferred_element_type=F32)
                acc = part if acc is None else acc + part
            att[rows, hs] = (acc * (1.0 / total)).astype(BF)
        return carry

    lax.fori_loop(0, ROWS // BLK, one_block, 0)
    for i in range(0, ROWS, 256):
        out[i : i + 256, :] = jnp.dot(
            att[i : i + 256, :], wo_buf[...], preferred_element_type=F32
        ).astype(BF)


def body(tokens, w_query, w_key, w_value, w_output, nbr_index, nbr_count):
    tok = tokens[0]
    dp = lax.axis_index("dp")
    rank = lax.axis_index("ctx")
    ylo, core, par = dp // 2, dp % 2, (rank // 16) % 2
    pos = jnp.stack([ylo, core, par]).astype(jnp.int32)

    up, down = ctx_routes(1), ctx_routes(-1)
    own = jnp.stack([w_key, w_value, w_query, w_output])
    half = lax.dynamic_slice_in_dim(own, par * 64, 64, axis=1)
    mine = jnp.stack([send(half, p) for p in (FROM_UP, FROM_DOWN, FROM_FAR)])
    low = send(tok, up)
    high = send(tok, down)
    sib = send(own, SIBLING)
    other_kv = send(mine[:, :2], X_NEXT)
    other_qo = send(mine[:, 2:], X_PREV)
    sib_mine = send(mine, SIBLING)
    sib_kv = send(other_kv, SIBLING)
    sib_qo = send(other_qo, SIBLING)
    low2 = send(low, up)
    high2 = send(high, down)

    vm = pl.BlockSpec(memory_space=pltpu.VMEM)
    anyspace = pl.BlockSpec(memory_space=pl.ANY)
    smem = pl.BlockSpec(memory_space=pltpu.SMEM)
    params = pltpu.CompilerParams(vmem_limit_bytes=VMEM_LIMIT)
    pieces_kv = (own, sib, mine, other_kv, sib_mine, sib_kv)
    pieces_qo = (own, sib, mine, other_qo, sib_mine, sib_qo)
    kv_own, w_kv = pl.pallas_call(
        first_proj_kernel,
        in_specs=[smem, vm] + [anyspace] * 6,
        out_specs=[vm, anyspace],
        out_shape=[
            jax.ShapeDtypeStruct((ROWS, 2 * D), BF),
            jax.ShapeDtypeStruct((D, 2 * D), BF),
        ],
        scratch_shapes=[
            pltpu.VMEM((D, 2 * D), BF),
            pltpu.SemaphoreType.DMA,
            pltpu.SemaphoreType.DMA,
        ],
        compiler_params=params,
        name="first_proj",
    )(pos, tok, *pieces_kv)

    kv_pair = pl.pallas_call(
        pair_kernel,
        grid=(4,),
        in_specs=[
            pl.BlockSpec((256, D), lambda i: (jnp.minimum(i, 1), 0)),
            pl.BlockSpec((256, D), lambda i: (jnp.maximum(i - 2, 0), 0)),
            pl.BlockSpec((D, 2 * D), lambda i: (0, 0), pipeline_mode=pl.Buffered(1)),
        ],
        out_specs=pl.BlockSpec((256, 2 * D), lambda i: (i, 0)),
        out_shape=jax.ShapeDtypeStruct((2 * ROWS, 2 * D), BF),
        compiler_params=params,
        name="pair",
    )(high, low, w_kv)
    query, w_o = pl.pallas_call(
        query_kernel,
        in_specs=[smem, vm] + [anyspace] * 6,
        out_specs=[vm, anyspace],
        out_shape=[jax.ShapeDtypeStruct((ROWS, D), BF), jax.ShapeDtypeStruct((D, D), BF)],
        scratch_shapes=[
            pltpu.VMEM((D, 2 * D), BF),
            pltpu.SemaphoreType.DMA,
            pltpu.SemaphoreType.DMA,
        ],
        compiler_params=params,
        name="query",
    )(pos, tok, *pieces_qo)
    index = nbr_index[0] - (rank * (ROWS // BLK) - REACH * (ROWS // BLK))
    update = pl.pallas_call(
        final_kernel,
        in_specs=[smem, smem, vm, vm, vm] + [anyspace] * 4,
        out_specs=vm,
        out_shape=jax.ShapeDtypeStruct((ROWS, D), BF),
        scratch_shapes=[
            pltpu.VMEM((5 * ROWS, 2 * D), BF),
            pltpu.VMEM((D, 2 * D), BF),
            pltpu.VMEM((D, D), BF),
            pltpu.VMEM((ROWS, D), BF),
            pltpu.VMEM((HEADS, BLK, MAXN * BLK), F32),
            pltpu.SemaphoreType.DMA((5,)),
        ],
        compiler_params=params,
        name="final",
    )(index, nbr_count[0], low2, high2, query, w_kv, w_o, kv_pair, kv_own)
    return update[None]


def solution(mesh):
    placed = (
        P("dp", "ctx", None),
        P("dp", None),
        P("dp", None),
        P("dp", None),
        P("dp", None),
        P("dp", "ctx", None),
        P("dp", "ctx"),
    )
    return jax.shard_map(
        body, mesh=mesh, in_specs=placed, out_specs=P("dp", "ctx", None), check_vma=False
    )
```

```python
import numpy as np
import jax
import jax.numpy as jnp
from jax import lax
from jax.experimental import pallas as pl
from jax.experimental.pallas import tpu as pltpu
from jax.sharding import PartitionSpec as P

D = 1024
HEADS = 8
HD = 128
BLK = 128
MAXN = 8
REACH = 2
ROWS = 512
NDP = 8
NCTX = 64
BF = jnp.bfloat16
F32 = jnp.float32
SCALE2 = float(HD ** (-0.5) * np.log2(np.e))
VMEM_LIMIT = 60 << 20
AXES = ("dp", "ctx")


def flat(x, y, z, core):
    return ((y % 4) * 2 + core) * NCTX + (x % 4) * 16 + ((y % 8) // 4) * 8 + z % 8


def coords(index):
    dp, ctx = divmod(index, NCTX)
    return ctx // 16, (ctx // 8 % 2) * 4 + dp // 2, ctx % 8, dp % 2


def routes(target):
    return [(i, flat(*target(*coords(i)))) for i in range(NDP * NCTX)]


def ctx_routes(step, keep=lambda r: True):
    return [
        (dp * NCTX + r, dp * NCTX + r + step)
        for dp in range(NDP)
        for r in range(NCTX)
        if 0 <= r + step < NCTX and keep(r)
    ]


FROM_UP = routes(lambda x, y, z, c: (x, y - 1, z, c))
FROM_DOWN = routes(lambda x, y, z, c: (x, y + 1, z, c))
FROM_FAR = routes(lambda x, y, z, c: (x, y + 2 if y % 2 == 0 else y - 2, z, c))
SHIFTS = (1, -1, 2)
X_NEXT = routes(lambda x, y, z, c: (x + 1, y, z, c))
X_PREV = routes(lambda x, y, z, c: (x - 1, y, z, c))
SIBLING = routes(lambda x, y, z, c: (x, y, z, 1 - c))


def send(value, pairs):
    return lax.ppermute(value, AXES, pairs)


def normalise(tok):
    v = tok.astype(F32)
    return (v * lax.rsqrt(jnp.mean(v * v, axis=-1, keepdims=True) + 1e-05)).astype(BF)


def piece_copies(pos, srcs, picks, dst, sem):
    ylo, core, par = pos[0], pos[1], pos[2]
    own, sib, mine, other, sib_mine, sib_other = srcs
    copies = []

    def add(src, row, n, col):
        copies.append(
            pltpu.make_async_copy(
                src, dst.at[pl.ds(pl.multiple_of(row, 64), n), pl.ds(col, D)], sem
            )
        )

    for at, w in enumerate(picks):
        add(own.at[w], (ylo * 2 + core) * 128, 128, at * D)
        add(sib.at[w], (ylo * 2 + 1 - core) * 128, 128, at * D)
        for i, s in enumerate(SHIFTS):
            base = lax.rem(ylo + s + 4, 4) * 2
            row = (base + core) * 128
            row_sib = (base + 1 - core) * 128
            add(mine.at[i, w], row + par * 64, 64, at * D)
            add(other.at[i, w % 2], row + (1 - par) * 64, 64, at * D)
            add(sib_mine.at[i, w], row_sib + par * 64, 64, at * D)
            add(sib_other.at[i, w % 2], row_sib + (1 - par) * 64, 64, at * D)
    return copies


def first_proj_kernel(pos, tok, *refs):
    srcs, (out, w_out, w_buf, sem, sem2) = refs[:6], refs[6:]
    copies = piece_copies(pos, srcs, (0, 1), w_buf, sem)
    for c in copies:
        c.start()
    normed = normalise(tok[...])
    for c in copies:
        c.wait()
    save = pltpu.make_async_copy(w_buf, w_out, sem2)
    save.start()
    out[...] = jnp.dot(normed, w_buf[...], preferred_element_type=F32).astype(BF)
    save.wait()


def pair_kernel(high, low, w, out):
    tok = jnp.where(pl.program_id(0) < 2, high[...], low[...])
    out[...] = jnp.dot(normalise(tok), w[...], preferred_element_type=F32).astype(BF)


def query_kernel(pos, tok, *refs):
    srcs, (out, w_out, w_buf, sem, sem2) = refs[:6], refs[6:]
    copies = piece_copies(pos, srcs, (2, 3), w_buf, sem)
    for c in copies:
        c.start()
    normed = normalise(tok[...])
    for c in copies:
        c.wait()
    save = pltpu.make_async_copy(w_buf.at[:, pl.ds(D, D)], w_out, sem2)
    save.start()
    out[...] = jnp.dot(normed, w_buf[:, :D], preferred_element_type=F32).astype(BF)
    save.wait()


def final_kernel(
    idx, cnt, low2, up2, query, w_kv, w_o, kv_pair, kv_own, out, kv, w_buf, wo_buf, att, score, sem
):
    get_w = pltpu.make_async_copy(w_kv, w_buf, sem.at[0])
    get_w.start()
    gets = [
        pltpu.make_async_copy(kv_pair.at[pl.ds(ROWS, ROWS)], kv.at[pl.ds(ROWS, ROWS)], sem.at[1]),
        pltpu.make_async_copy(kv_own, kv.at[pl.ds(2 * ROWS, ROWS)], sem.at[2]),
        pltpu.make_async_copy(kv_pair.at[pl.ds(0, ROWS)], kv.at[pl.ds(3 * ROWS, ROWS)], sem.at[3]),
    ]
    gets.append(pltpu.make_async_copy(w_o, wo_buf, sem.at[4]))
    for g in gets:
        g.start()
    normed = [normalise(low2[...]), normalise(up2[...])]
    get_w.wait()
    for tok, base in zip(normed, (0, 4 * ROWS)):
        kv[base : base + ROWS, :] = jnp.dot(
            tok, w_buf[...], preferred_element_type=F32
        ).astype(BF)
    for g in gets:
        g.wait()

    def one_block(b, carry):
        used = cnt[b]
        rows = pl.ds(pl.multiple_of(b * BLK, BLK), BLK)
        starts = [
            pl.multiple_of(jnp.where(j < used, idx[b, j], idx[b, 0]) * BLK, BLK)
            for j in range(MAXN)
        ]
        bias = [jnp.where(j < used, 0.0, -1e30) for j in range(MAXN)]
        for h in range(HEADS):
            hs = pl.ds(h * HD, HD)
            q = query[rows, hs]
            for j in range(MAXN):
                score[h, :, j * BLK : (j + 1) * BLK] = lax.dot_general(
                    q, kv[pl.ds(starts[j], BLK), hs], (((1,), (1,)), ((), ())),
                    preferred_element_type=F32,
                )
        for h in range(HEADS):
            hs = pl.ds(h * HD, HD)
            scores = [score[h, :, j * BLK : (j + 1) * BLK] for j in range(MAXN)]
            peak = scores[0]
            for s in scores[1:]:
                peak = jnp.maximum(peak, s)
            peak = jnp.max(peak, axis=-1, keepdims=True)
            expo = [jnp.exp2((s - (peak - off)) * SCALE2) for s, off in zip(scores, bias)]
            total = expo[0]
            for e in expo[1:]:
                total = total + e
            total = jnp.sum(total, axis=-1, keepdims=True)
            acc = None
            for j in range(0, MAXN, 2):
                vals = jnp.concatenate(
                    [kv[pl.ds(starts[i], BLK), pl.ds(D + h * HD, HD)] for i in (j, j + 1)], axis=0
                )
                wts = jnp.concatenate([expo[j].astype(BF), expo[j + 1].astype(BF)], axis=1)
                part = jnp.dot(wts, vals, preferred_element_type=F32)
                acc = part if acc is None else acc + part
            att[rows, hs] = (acc * (1.0 / total)).astype(BF)
        return carry

    lax.fori_loop(0, ROWS // BLK, one_block, 0)
    for i in range(0, ROWS, 256):
        out[i : i + 256, :] = jnp.dot(
            att[i : i + 256, :], wo_buf[...], preferred_element_type=F32
        ).astype(BF)


def body(tokens, w_query, w_key, w_value, w_output, nbr_index, nbr_count):
    tok = tokens[0]
    dp = lax.axis_index("dp")
    rank = lax.axis_index("ctx")
    ylo, core, par = dp // 2, dp % 2, (rank // 16) % 2
    pos = jnp.stack([ylo, core, par]).astype(jnp.int32)

    up, down = ctx_routes(1), ctx_routes(-1)
    own = jnp.stack([w_key, w_value, w_query, w_output])
    half = lax.dynamic_slice_in_dim(own, par * 64, 64, axis=1)
    mine = jnp.stack([send(half, p) for p in (FROM_UP, FROM_DOWN, FROM_FAR)])
    low = send(tok, up)
    high = send(tok, down)
    sib = send(own, SIBLING)
    other_kv = send(mine[:, :2], X_NEXT)
    other_qo = send(mine[:, 2:], X_PREV)
    sib_mine = send(mine, SIBLING)
    sib_kv = send(other_kv, SIBLING)
    sib_qo = send(other_qo, SIBLING)
    low2 = send(low, up)
    high2 = send(high, down)

    vm = pl.BlockSpec(memory_space=pltpu.VMEM)
    anyspace = pl.BlockSpec(memory_space=pl.ANY)
    smem = pl.BlockSpec(memory_space=pltpu.SMEM)
    params = pltpu.CompilerParams(vmem_limit_bytes=VMEM_LIMIT)
    pieces_kv = (own, sib, mine, other_kv, sib_mine, sib_kv)
    pieces_qo = (own, sib, mine, other_qo, sib_mine, sib_qo)
    kv_own, w_kv = pl.pallas_call(
        first_proj_kernel,
        in_specs=[smem, vm] + [anyspace] * 6,
        out_specs=[vm, anyspace],
        out_shape=[
            jax.ShapeDtypeStruct((ROWS, 2 * D), BF),
            jax.ShapeDtypeStruct((D, 2 * D), BF),
        ],
        scratch_shapes=[
            pltpu.VMEM((D, 2 * D), BF),
            pltpu.SemaphoreType.DMA,
            pltpu.SemaphoreType.DMA,
        ],
        compiler_params=params,
        name="first_proj",
    )(pos, tok, *pieces_kv)

    kv_pair = pl.pallas_call(
        pair_kernel,
        grid=(4,),
        in_specs=[
            pl.BlockSpec((256, D), lambda i: (jnp.minimum(i, 1), 0)),
            pl.BlockSpec((256, D), lambda i: (jnp.maximum(i - 2, 0), 0)),
            pl.BlockSpec((D, 2 * D), lambda i: (0, 0), pipeline_mode=pl.Buffered(1)),
        ],
        out_specs=pl.BlockSpec((256, 2 * D), lambda i: (i, 0)),
        out_shape=jax.ShapeDtypeStruct((2 * ROWS, 2 * D), BF),
        compiler_params=params,
        name="pair",
    )(high, low, w_kv)
    query, w_o = pl.pallas_call(
        query_kernel,
        in_specs=[smem, vm] + [anyspace] * 6,
        out_specs=[vm, anyspace],
        out_shape=[jax.ShapeDtypeStruct((ROWS, D), BF), jax.ShapeDtypeStruct((D, D), BF)],
        scratch_shapes=[
            pltpu.VMEM((D, 2 * D), BF),
            pltpu.SemaphoreType.DMA,
            pltpu.SemaphoreType.DMA,
        ],
        compiler_params=params,
        name="query",
    )(pos, tok, *pieces_qo)
    index = nbr_index[0] - (rank * (ROWS // BLK) - REACH * (ROWS // BLK))
    update = pl.pallas_call(
        final_kernel,
        in_specs=[smem, smem, vm, vm, vm] + [anyspace] * 4,
        out_specs=vm,
        out_shape=jax.ShapeDtypeStruct((ROWS, D), BF),
        scratch_shapes=[
            pltpu.VMEM((5 * ROWS, 2 * D), BF),
            pltpu.VMEM((D, 2 * D), BF),
            pltpu.VMEM((D, D), BF),
            pltpu.VMEM((ROWS, D), BF),
            pltpu.VMEM((HEADS, BLK, MAXN * BLK), F32),
            pltpu.SemaphoreType.DMA((5,)),
        ],
        compiler_params=params,
        name="final",
    )(index, nbr_count[0], low2, high2, query, w_kv, w_o, kv_pair, kv_own)
    return update[None]


def solution(mesh):
    placed = (
        P("dp", "ctx", None),
        P("dp", None),
        P("dp", None),
        P("dp", None),
        P("dp", None),
        P("dp", "ctx", None),
        P("dp", "ctx"),
    )
    return jax.shard_map(
        body, mesh=mesh, in_specs=placed, out_specs=P("dp", "ctx", None), check_vma=False
    )
```
